32 devices in a mesh: fsdp: 4 (over x, core), context: 4 (over z), tensor: 2 (over y).
Axes of the slice: x: 2, y: 2, z: 4, core: 2. Of those that a mesh axis runs over, the one named last changes fastest.
Arguments:
- x_in: bfloat16 [2560, 2304], P(('fsdp', 'context')), may hold values from -6 to 6
- doc_lengths: int32 [4, 4], P('fsdp'), may hold values from 1 to 576, 640 in all within a row
- w_query: bfloat16 [2304, 2048], P(('fsdp', 'context'), 'tensor'), may hold values from -0.125 to 0.125
- key_weight: bfloat16 [2304, 1024], P(('fsdp', 'context'), 'tensor'), may hold values from -0.125 to 0.125
- value_weight: bfloat16 [2304, 1024], P(('fsdp', 'context'), 'tensor'), may hold values from -0.125 to 0.125
- output_weight: bfloat16 [2304, 2048], P(('fsdp', 'context'), 'tensor'), may hold values from -0.125 to 0.125
- w_gate: bfloat16 [2304, 9216], P(('fsdp', 'context'), 'tensor'), may hold values from -0.125 to 0.125
- w_up: bfloat16 [2304, 9216], P(('fsdp', 'context'), 'tensor'), may hold values from -0.125 to 0.125
- w_down: bfloat16 [2304, 9216], P(('fsdp', 'context'), 'tensor'), may hold values from -0.0625 to 0.0625
- norm_gains: bfloat16 [2304, 4], P(('fsdp', 'context')), may hold values from 0.099609375 to 1.8984375
- grad_y: bfloat16 [2560, 2304], P(('fsdp', 'context')), may hold values from -6 to 6
Outputs:
- y_out: bfloat16 [2560, 2304], P(('fsdp', 'context'))
- grad_x: bfloat16 [2560, 2304], P(('fsdp', 'context'))
- grad_w_query: float32 [2304, 2048], P(('fsdp', 'context'), 'tensor')
- grad_w_key: float32 [2304, 1024], P(('fsdp', 'context'), 'tensor')
- grad_w_value: float32 [2304, 1024], P(('fsdp', 'context'), 'tensor')
- grad_w_out: float32 [2304, 2048], P(('fsdp', 'context'), 'tensor')
- grad_w_gate: float32 [2304, 9216], P(('fsdp', 'context'), 'tensor')
- grad_w_up: float32 [2304, 9216], P(('fsdp', 'context'), 'tensor')
- grad_w_down: float32 [2304, 9216], P(('fsdp', 'context'), 'tensor')
- grad_gains: float32 [2304, 4], P(('fsdp', 'context'))
The draws below stay inside these ranges and needn't reach their ends.
Inputs may be any that keep to these rules, and one draw needn't show every extreme that they name: `doc_lengths`: each row lists the lengths of one sequence's 4 documents in order; they sum to 640, and the longest is exactly 576.
All inputs are finite; a program needn't handle non-finite values.
Results may differ from the reference program's by a relative error of at most 0.02.
Values may be sent and summed in bfloat16 or wider, within the bound.
No kernel may reach another device: no remote copies, remote signals or barrier semaphores. Data moves between devices by JAX's collectives and lax.ppermute only.
A program may use at most 576 MiB of HBM per device.

```python
import math
import jax
import jax.numpy as jnp
import numpy as np
from jax import lax

MODEL_WIDTH = 2304
QUERY_HEADS = 8
KEY_VALUE_HEADS = 4
HEAD_SIZE = 256
FF = 9216
WINDOW = 4096
DOCS = 4
TOK_DEV = 160
SEQ_LEN = 640
TOKENS = 2560
DOC_MOST = 576
N_FSDP = 4


def steps_of(own_key, shape, split, smallest, high):
    def one(dim, parts):
        draws = jax.random.uniform(jax.random.fold_in(jax.random.fold_in(own_key, 6), dim), (parts,), jnp.float32, smallest / len(split), high / len(split))
        return jnp.repeat(jnp.exp(draws), shape[dim] // parts).reshape((-1,) + (1,) * (len(shape) - dim - 1))

    level = one(*split[0])
    for cut in split[1:]:
        level = level * one(*cut)
    return level


def split_up(amount, total, limit, skew):
    weights = [(1 << 20) // math.isqrt(standing ** skew) + 1 for standing in range(2, amount + 1)]
    surplus, holding = total - limit - (amount - 1), [1] * (amount - 1)
    while surplus > 0:
        movable = [i for i in range(amount - 1) if holding[i] < limit]
        mass, remaining = sum([weights[i] for i in movable]), surplus
        for i in movable:
            addition = min(limit - holding[i], max(1, remaining * weights[i] // mass), surplus)
            holding[i] = holding[i] + addition
            surplus = surplus - addition
    return np.array([limit] + holding)


def uneven(key, number_of, total, reach, skew):
    if number_of == 2:
        one = jax.random.randint(key, (), max(1, total - reach), min(reach, total - 1) + 1)
        return jnp.stack([one, total - one])
    tallies = jnp.asarray(split_up(number_of, total, reach, skew), jnp.int32)
    twos = (number_of - 1) // 2
    giver, receiver = tallies[1:1 + 2 * twos:2], tallies[2:2 + 2 * twos:2]
    slack = jnp.minimum(giver - 1, reach - receiver)
    moved = jax.random.randint(jax.random.fold_in(key, 1), (twos,), 0, 1 << 20) % (slack + 1)
    tallies = tallies.at[1:1 + 2 * twos:2].set(giver - moved).at[2:2 + 2 * twos:2].set(receiver + moved)
    return tallies[jax.random.permutation(jax.random.fold_in(key, 2), number_of)]


def scatter_about(stream_key, dims, scale, most, shards=(), kind=jnp.bfloat16):
    gain = steps_of(stream_key, dims, shards, -0.22, 0.18) if shards else 1.0
    drawn = jax.random.normal(stream_key, dims, jnp.float32) * scale * gain
    return jnp.minimum(jnp.maximum(drawn, -most), most).astype(kind)


def setup_inputs(seed: int = 0) -> dict:
    arg_keys = jax.random.split(jax.random.key(seed), 12)
    x_in = scatter_about(arg_keys[0], (TOKENS, MODEL_WIDTH), 1.0, 6.0, ((0, 16),))
    doc_lengths = jax.vmap(lambda own: uneven(own, DOCS, SEQ_LEN, DOC_MOST, 2))(jax.random.split(arg_keys[1], N_FSDP)).reshape((N_FSDP, DOCS)).astype(jnp.int32)
    w_query = scatter_about(arg_keys[2], (MODEL_WIDTH, QUERY_HEADS * HEAD_SIZE), MODEL_WIDTH ** -0.5, 0.125, ((0, 16), (1, 2)))
    key_weight = scatter_about(arg_keys[3], (MODEL_WIDTH, KEY_VALUE_HEADS * HEAD_SIZE), MODEL_WIDTH ** -0.5, 0.125, ((0, 16), (1, 2)))
    value_weight = scatter_about(arg_keys[4], (MODEL_WIDTH, KEY_VALUE_HEADS * HEAD_SIZE), MODEL_WIDTH ** -0.5, 0.125, ((0, 16), (1, 2)))
    output_weight = scatter_about(arg_keys[5], (MODEL_WIDTH, QUERY_HEADS * HEAD_SIZE), (QUERY_HEADS * HEAD_SIZE) ** -0.5, 0.125, ((0, 16), (1, 2)))
    w_gate = scatter_about(arg_keys[6], (MODEL_WIDTH, FF), MODEL_WIDTH ** -0.5, 0.125, ((0, 16), (1, 2)))
    w_up = scatter_about(arg_keys[7], (MODEL_WIDTH, FF), MODEL_WIDTH ** -0.5, 0.125, ((0, 16), (1, 2)))
    w_down = scatter_about(arg_keys[8], (MODEL_WIDTH, FF), FF ** -0.5, 0.0625, ((0, 16), (1, 2)))
    norm_gains = jnp.clip(1.0 + 0.18 * jax.random.normal(arg_keys[9], (MODEL_WIDTH, 4), jnp.float32), 0.099609375, 1.8984375).astype(jnp.bfloat16)
    grad_y = scatter_about(arg_keys[10], (TOKENS, MODEL_WIDTH), 1.0, 6.0, ((0, 16),))
    return {"x_in": x_in, "doc_lengths": doc_lengths, "w_query": w_query, "key_weight": key_weight, "value_weight": value_weight, "output_weight": output_weight, "w_gate": w_gate, "w_up": w_up, "w_down": w_down, "norm_gains": norm_gains, "grad_y": grad_y}


EPSILON = 1e-06
SOFT_CAP = 50.0
SCORE_SCALE = 0.0625
ROPE_BASE = 10000.0
GELU_ROOT = 0.7978845608028654
GELU_CUBE = 0.044715

def cast_bfloat(value_rows_list):
    return lax.optimization_barrier(value_rows_list.astype(jnp.bfloat16))

def segment_info(lengths, tok_ids):
    doc_ends = jnp.cumsum(lengths).astype(jnp.int32)
    doc_starts = (doc_ends - lengths).astype(jnp.int32)
    segment = lax.optimization_barrier(jnp.sum((tok_ids[:, None] >= doc_ends[None, :]).astype(jnp.int32), axis=1)).astype(jnp.int32)
    doc_ids = jnp.arange(lengths.shape[0], dtype=jnp.int32)
    picked = jnp.where(segment[:, None] == doc_ids[None, :], doc_starts[None, :], 0)
    position = (tok_ids - lax.optimization_barrier(jnp.sum(picked, axis=1))).astype(jnp.int32)
    return (segment, position)

def rope_tables(position, half_dim):
    exponent = jnp.arange(half_dim, dtype=jnp.float32) * (2.0 / (2 * half_dim))
    frequency = ROPE_BASE ** (-exponent)
    angles = position.astype(jnp.float32)[:, None] * frequency[None, :]
    return (jnp.cos(angles), jnp.sin(angles))

def apply_rotary(tensor, cosine_table, sine_table):
    half_dim = tensor.shape[-1] // 2
    lower, upper = (tensor[..., :half_dim], tensor[..., half_dim:])
    cos_b, sin_b = (cosine_table[:, None, :], sine_table[:, None, :])
    return jnp.concatenate([lower * cos_b - upper * sin_b, upper * cos_b + lower * sin_b], axis=-1)

def rotary_backward(tensor, cosine_table, sine_table):
    half_dim = tensor.shape[-1] // 2
    lower, upper = (tensor[..., :half_dim], tensor[..., half_dim:])
    cos_b, sin_b = (cosine_table[:, None, :], sine_table[:, None, :])
    return jnp.concatenate([lower * cos_b + upper * sin_b, upper * cos_b - lower * sin_b], axis=-1)

def rms_unit(value_rows_list):
    inv_rms = lax.rsqrt(lax.optimization_barrier(jnp.mean(value_rows_list * value_rows_list, axis=-1, keepdims=True)) + EPSILON)
    return (value_rows_list * inv_rms, inv_rms)

def norm_back(cotangent, normed, inv_rms, gain_col):
    scaled = cotangent * gain_col[None, :]
    return inv_rms * (scaled - normed * lax.optimization_barrier(jnp.mean(scaled * normed, axis=-1, keepdims=True)))

def gelu_parts(value_rows_list):
    tangent = jnp.tanh(GELU_ROOT * (value_rows_list + GELU_CUBE * value_rows_list * value_rows_list * value_rows_list))
    result = 0.5 * value_rows_list * (1.0 + tangent)
    slope = 0.5 * (1.0 + tangent) + 0.5 * value_rows_list * (1.0 - tangent * tangent) * GELU_ROOT * (1.0 + 3.0 * GELU_CUBE * value_rows_list * value_rows_list)
    return (result, slope)

def live_pairs(query_seg, query_tok, key_seg, key_tok):
    same_doc = query_seg[:, None] == key_seg[None, :]
    causal = key_tok[None, :] <= query_tok[:, None]
    inside = query_tok[:, None] - key_tok[None, :] < WINDOW
    return same_doc & causal & inside

def capped_scores(query_rows_rotated, key_rows):
    raw_dot = jnp.einsum('qhgd,khd->hgqk', query_rows_rotated.astype(jnp.float32), key_rows.astype(jnp.float32))
    return SOFT_CAP * jnp.tanh(raw_dot * SCORE_SCALE / SOFT_CAP)

def sequence_pass(x_seq, lengths, dy_seq, w_query, key_weight, value_weight, output_weight, w_gate, w_up, w_down, norm_gains):
    sequence_row_list = x_seq.shape[0]
    query_groups = QUERY_HEADS // KEY_VALUE_HEADS
    block_rows = 4 * TOK_DEV
    block_count = sequence_row_list // block_rows
    tok_ids = jnp.arange(sequence_row_list, dtype=jnp.int32)
    segment, position = segment_info(lengths, tok_ids)
    cosine_table, sine_table = rope_tables(position, HEAD_SIZE // 2)
    gain_f = norm_gains.astype(jnp.float32)
    x_f32 = x_seq.astype(jnp.float32)
    normed1, inv_rms1 = rms_unit(x_f32)
    attention_input_rows = cast_bfloat(normed1 * gain_f[:, 0][None, :])
    projected_queries = jnp.dot(attention_input_rows, w_query, preferred_element_type=jnp.float32).reshape(sequence_row_list, QUERY_HEADS, HEAD_SIZE)
    projected_keys = jnp.dot(attention_input_rows, key_weight, preferred_element_type=jnp.float32).reshape(sequence_row_list, KEY_VALUE_HEADS, HEAD_SIZE)
    value_rows_list = cast_bfloat(jnp.dot(attention_input_rows, value_weight, preferred_element_type=jnp.float32)).reshape(sequence_row_list, KEY_VALUE_HEADS, HEAD_SIZE)
    query_rows_rotated = cast_bfloat(apply_rotary(projected_queries, cosine_table, sine_table)).reshape(sequence_row_list, KEY_VALUE_HEADS, query_groups, HEAD_SIZE)
    key_rows = cast_bfloat(apply_rotary(projected_keys, cosine_table, sine_table))

    def forward_block(block_index):
        begin = (block_index * block_rows).astype(jnp.int32)
        query_blk = lax.dynamic_slice_in_dim(query_rows_rotated, begin, block_rows, 0)
        seg_blk = lax.dynamic_slice_in_dim(segment, begin, block_rows, 0)
        tok_blk = lax.dynamic_slice_in_dim(tok_ids, begin, block_rows, 0)
        capped = capped_scores(query_blk, key_rows)
        allowed = live_pairs(seg_blk, tok_blk, segment, tok_ids)[None, None]
        raw_weight = jnp.where(allowed, jnp.exp(capped - SOFT_CAP), 0.0)
        denom = lax.optimization_barrier(jnp.sum(raw_weight, axis=-1))
        accum = jnp.einsum('hgqk,khd->qhgd', cast_bfloat(raw_weight).astype(jnp.float32), value_rows_list.astype(jnp.float32))
        result = cast_bfloat(accum / jnp.transpose(denom, (2, 0, 1))[..., None])
        return (result, SOFT_CAP + jnp.log(denom))
    attention_block_list, log_blocks = lax.map(forward_block, jnp.arange(block_count, dtype=jnp.int32))
    attention_output_rows = attention_block_list.reshape(sequence_row_list, KEY_VALUE_HEADS, query_groups, HEAD_SIZE)
    out_flat = attention_output_rows.reshape(sequence_row_list, QUERY_HEADS * HEAD_SIZE)
    branch = jnp.dot(out_flat, output_weight.T, preferred_element_type=jnp.float32)
    normed2, inv_rms2 = rms_unit(branch)
    resid = x_f32 + normed2 * gain_f[:, 1][None, :]
    normed3, inv_rms3 = rms_unit(resid)
    ffn_input = cast_bfloat(normed3 * gain_f[:, 2][None, :])
    gate = jnp.dot(ffn_input, w_gate, preferred_element_type=jnp.float32)
    upward = jnp.dot(ffn_input, w_up, preferred_element_type=jnp.float32)
    gelu_value, gelu_slope = gelu_parts(gate)
    hidden = cast_bfloat(gelu_value * upward)
    mix = jnp.dot(hidden, w_down.T, preferred_element_type=jnp.float32)
    normed4, inv_rms4 = rms_unit(mix)
    y_seq = (resid + normed4 * gain_f[:, 3][None, :]).astype(jnp.bfloat16)
    dy_f32 = dy_seq.astype(jnp.float32)
    dgain4 = lax.optimization_barrier(jnp.sum(dy_f32 * normed4, axis=0))
    dmix = cast_bfloat(norm_back(dy_f32, normed4, inv_rms4, gain_f[:, 3]))
    dhidden = jnp.dot(dmix, w_down, preferred_element_type=jnp.float32)
    grad_down = jnp.dot(dmix.T, hidden, preferred_element_type=jnp.float32)
    dgate = cast_bfloat(dhidden * upward * gelu_slope)
    dupward = cast_bfloat(dhidden * gelu_value)
    dffn = jnp.dot(dgate, w_gate.T, preferred_element_type=jnp.float32) + jnp.dot(dupward, w_up.T, preferred_element_type=jnp.float32)
    grad_gate = jnp.dot(ffn_input.T, dgate, preferred_element_type=jnp.float32)
    grad_up = jnp.dot(ffn_input.T, dupward, preferred_element_type=jnp.float32)
    dgain3 = lax.optimization_barrier(jnp.sum(dffn * normed3, axis=0))
    dresid = dy_f32 + norm_back(dffn, normed3, inv_rms3, gain_f[:, 2])
    dgain2 = lax.optimization_barrier(jnp.sum(dresid * normed2, axis=0))
    branch_gradient = cast_bfloat(norm_back(dresid, normed2, inv_rms2, gain_f[:, 1]))
    attention_output_gradient = jnp.dot(branch_gradient, output_weight, preferred_element_type=jnp.float32).reshape(sequence_row_list, KEY_VALUE_HEADS, query_groups, HEAD_SIZE)
    grad_out = jnp.dot(branch_gradient.T, out_flat, preferred_element_type=jnp.float32)
    dattn_b = cast_bfloat(attention_output_gradient)
    delta = lax.optimization_barrier(jnp.sum(attention_output_gradient * attention_output_rows.astype(jnp.float32), axis=-1))

    def backward_block(totals, block_index):
        dkey_sum, dval_sum = totals
        begin = (block_index * block_rows).astype(jnp.int32)
        query_blk = lax.dynamic_slice_in_dim(query_rows_rotated, begin, block_rows, 0)
        seg_blk = lax.dynamic_slice_in_dim(segment, begin, block_rows, 0)
        tok_blk = lax.dynamic_slice_in_dim(tok_ids, begin, block_rows, 0)
        grad_blk = lax.dynamic_slice_in_dim(dattn_b, begin, block_rows, 0)
        delta_blk = jnp.transpose(lax.dynamic_slice_in_dim(delta, begin, block_rows, 0), (1, 2, 0))
        log_blk = log_blocks[block_index]
        capped = capped_scores(query_blk, key_rows)
        allowed = live_pairs(seg_blk, tok_blk, segment, tok_ids)[None, None]
        prob = jnp.where(allowed, jnp.exp(capped - log_blk[..., None]), 0.0)
        dprob = jnp.einsum('qhgd,khd->hgqk', grad_blk.astype(jnp.float32), value_rows_list.astype(jnp.float32))
        dscore = prob * (dprob - delta_blk[..., None])
        dscore_b = cast_bfloat(dscore * (1.0 - (capped / SOFT_CAP) ** 2) * SCORE_SCALE).astype(jnp.float32)
        prob_b = cast_bfloat(prob).astype(jnp.float32)
        dquery = jnp.einsum('hgqk,khd->qhgd', dscore_b, key_rows.astype(jnp.float32))
        dkey_sum = dkey_sum + jnp.einsum('hgqk,qhgd->khd', dscore_b, query_blk.astype(jnp.float32))
        dval_sum = dval_sum + jnp.einsum('hgqk,qhgd->khd', prob_b, grad_blk.astype(jnp.float32))
        return ((dkey_sum, dval_sum), dquery)
    initial_gradient_sums = (jnp.zeros((sequence_row_list, KEY_VALUE_HEADS, HEAD_SIZE), jnp.float32), jnp.zeros((sequence_row_list, KEY_VALUE_HEADS, HEAD_SIZE), jnp.float32))
    key_gradient_sums, dquery_blocks = lax.scan(backward_block, initial_gradient_sums, jnp.arange(block_count, dtype=jnp.int32))
    dqueries = dquery_blocks.reshape(sequence_row_list, QUERY_HEADS, HEAD_SIZE)
    dq_in = cast_bfloat(rotary_backward(dqueries, cosine_table, sine_table)).reshape(sequence_row_list, QUERY_HEADS * HEAD_SIZE)
    key_input_gradient = cast_bfloat(rotary_backward(key_gradient_sums[0], cosine_table, sine_table)).reshape(sequence_row_list, KEY_VALUE_HEADS * HEAD_SIZE)
    value_input_gradient = cast_bfloat(key_gradient_sums[1]).reshape(sequence_row_list, KEY_VALUE_HEADS * HEAD_SIZE)
    dinput = jnp.dot(dq_in, w_query.T, preferred_element_type=jnp.float32) + jnp.dot(key_input_gradient, key_weight.T, preferred_element_type=jnp.float32) + jnp.dot(value_input_gradient, value_weight.T, preferred_element_type=jnp.float32)
    grad_query = jnp.dot(attention_input_rows.T, dq_in, preferred_element_type=jnp.float32)
    grad_key = jnp.dot(attention_input_rows.T, key_input_gradient, preferred_element_type=jnp.float32)
    grad_value = jnp.dot(attention_input_rows.T, value_input_gradient, preferred_element_type=jnp.float32)
    dgain1 = lax.optimization_barrier(jnp.sum(dinput * normed1, axis=0))
    dx_seq = (dresid + norm_back(dinput, normed1, inv_rms1, gain_f[:, 0])).astype(jnp.bfloat16)
    grad_gain = jnp.stack([dgain1, dgain2, dgain3, dgain4], axis=1)
    grads = (grad_query, grad_key, grad_value, grad_out, grad_gate, grad_up, grad_down, grad_gain)
    return (y_seq, dx_seq, grads)

def reference(x_in, doc_lengths, w_query, key_weight, value_weight, output_weight, w_gate, w_up, w_down, norm_gains, grad_y):
    width = x_in.shape[1]
    x_seqs = x_in.reshape(N_FSDP, SEQ_LEN, width)
    dy_seqs = grad_y.reshape(N_FSDP, SEQ_LEN, width)

    def one_sequence(totals, inputs):
        x_seq, lengths, dy_seq = inputs
        y_seq, dx_seq, grads = sequence_pass(x_seq, lengths, dy_seq, w_query, key_weight, value_weight, output_weight, w_gate, w_up, w_down, norm_gains)
        return (jax.tree.map(lambda left, right: left + right, totals, grads), (y_seq, dx_seq))
    start_totals = (jnp.zeros(w_query.shape, jnp.float32), jnp.zeros(key_weight.shape, jnp.float32), jnp.zeros(value_weight.shape, jnp.float32), jnp.zeros(output_weight.shape, jnp.float32), jnp.zeros(w_gate.shape, jnp.float32), jnp.zeros(w_up.shape, jnp.float32), jnp.zeros(w_down.shape, jnp.float32), jnp.zeros((width, 4), jnp.float32))
    totals, outputs = lax.scan(one_sequence, start_totals, (x_seqs, doc_lengths, dy_seqs))
    y_out = outputs[0].reshape(N_FSDP * SEQ_LEN, width)
    grad_x = outputs[1].reshape(N_FSDP * SEQ_LEN, width)
    return (y_out, grad_x, totals[0], totals[1], totals[2], totals[3], totals[4], totals[5], totals[6], totals[7])
```

```python
import jax
import jax.numpy as jnp
from jax import lax
from jax.sharding import PartitionSpec as P

HEAD_SIZE = 256
WINDOW = 4096


EPSILON = 1e-06
SOFT_CAP = 50.0
SCORE_SCALE = 0.0625
ROPE_BASE = 10000.0
GELU_ROOT = 0.7978845608028654
GELU_CUBE = 0.044715
CONTRACT_ROWS = (((0,), (0,)), ((), ()))
CONTRACT_COLS = (((1,), (1,)), ((), ()))


def segment_info(lengths, tok_ids):
    doc_ends = jnp.cumsum(lengths)
    doc_starts = doc_ends - lengths
    segment = jnp.sum((tok_ids[:, None] >= doc_ends[None, :]).astype(jnp.int32), axis=1)
    doc_ids = jnp.arange(lengths.shape[0], dtype=jnp.int32)
    picked = jnp.where(segment[:, None] == doc_ids[None, :], doc_starts[None, :], 0)
    position = tok_ids - jnp.sum(picked, axis=1)
    return (segment, position)


def rope_tables(position, half_dim):
    exponent = jnp.arange(half_dim, dtype=jnp.float32) * (2.0 / (2 * half_dim))
    frequency = ROPE_BASE ** (-exponent)
    angles = position.astype(jnp.float32)[:, None] * frequency[None, :]
    return (jnp.cos(angles), jnp.sin(angles))


def apply_rotary(tensor, cosine_table, sine_table):
    half_dim = tensor.shape[-1] // 2
    lower, upper = (tensor[..., :half_dim], tensor[..., half_dim:])
    cos_b, sin_b = (cosine_table[:, None, :], sine_table[:, None, :])
    return jnp.concatenate([lower * cos_b - upper * sin_b, upper * cos_b + lower * sin_b], axis=-1)


def rotary_backward(tensor, cosine_table, sine_table):
    half_dim = tensor.shape[-1] // 2
    lower, upper = (tensor[..., :half_dim], tensor[..., half_dim:])
    cos_b, sin_b = (cosine_table[:, None, :], sine_table[:, None, :])
    return jnp.concatenate([lower * cos_b + upper * sin_b, upper * cos_b - lower * sin_b], axis=-1)


def rms_unit(value_rows_list):
    inv_rms = lax.rsqrt(
        jnp.mean(value_rows_list * value_rows_list, axis=-1, keepdims=True) + EPSILON
    )
    return (value_rows_list * inv_rms, inv_rms)


def norm_back(cotangent, normed, inv_rms, gain_col):
    scaled = cotangent * gain_col[None, :]
    return inv_rms * (scaled - normed * jnp.mean(scaled * normed, axis=-1, keepdims=True))


def gelu_parts(value_rows_list):
    tangent = jnp.tanh(
        GELU_ROOT
        * (value_rows_list + GELU_CUBE * value_rows_list * value_rows_list * value_rows_list)
    )
    result = 0.5 * value_rows_list * (1.0 + tangent)
    slope = 0.5 * (1.0 + tangent) + 0.5 * value_rows_list * (
        1.0 - tangent * tangent
    ) * GELU_ROOT * (1.0 + 3.0 * GELU_CUBE * value_rows_list * value_rows_list)
    return (result, slope)


def live_pairs(query_seg, query_tok, key_seg, key_tok):
    same_doc = query_seg[:, None] == key_seg[None, :]
    causal = key_tok[None, :] <= query_tok[:, None]
    inside = query_tok[:, None] - key_tok[None, :] < WINDOW
    return same_doc & causal & inside


def capped_scores(query_rows_rotated, key_rows):
    raw_dot = jnp.einsum(
        "qhgd,khd->hgqk", query_rows_rotated, key_rows, preferred_element_type=jnp.float32
    )
    return SOFT_CAP * jnp.tanh(raw_dot * SCORE_SCALE / SOFT_CAP)


def pick(options, index):
    chosen = options[0]
    for place in range(1, len(options)):
        chosen = jnp.where(index == place, options[place], chosen)
    return chosen


def swaps(count, step):
    return [(place, place ^ step) for place in range(count)]


def spread_columns(weight):
    count = lax.axis_size("context")
    part = weight.shape[1] // count
    if count != 4:
        return lax.all_to_all(weight, "context", split_axis=1, concat_axis=0, tiled=True)
    place = lax.axis_index("context")
    pieces = []
    for step in range(count):
        piece = lax.dynamic_slice_in_dim(weight, (place ^ step) * part, part, axis=1)
        pieces.append(lax.ppermute(piece, "context", swaps(count, step)) if step else piece)
    return jnp.concatenate([pick(pieces, place ^ row) for row in range(count)], axis=0)


def join_rows(rows):
    count = lax.axis_size("fsdp")
    if count != 4:
        return lax.all_gather(rows, "fsdp", axis=0, tiled=True)
    place = lax.axis_index("fsdp")
    far = lax.ppermute(rows, "fsdp", swaps(count, 2))
    near = lax.ppermute(rows, "fsdp", swaps(count, 1))
    cross = lax.ppermute(far, "fsdp", swaps(count, 1))
    pieces = [rows, near, far, cross]
    return jnp.concatenate([pick(pieces, place ^ row) for row in range(count)], axis=0)


def fetch_hidden(weight):
    return join_rows(spread_columns(weight))


def return_hidden(gradient):
    f_count, c_count = lax.axis_size("fsdp"), lax.axis_size("context")
    width, part = gradient.shape
    if f_count != 4 or c_count != 4:
        mine = lax.psum_scatter(
            gradient.astype(jnp.bfloat16), "fsdp", scatter_dimension=0, tiled=True
        )
        return lax.all_to_all(mine, "context", split_axis=0, concat_axis=1, tiled=True).astype(
            jnp.float32
        )
    f_place, c_place = lax.axis_index("fsdp"), lax.axis_index("context")
    block = width // f_count

    def of_member(step):
        return lax.dynamic_slice_in_dim(gradient, (f_place ^ step) * block, block, axis=0)

    near = lax.ppermute(of_member(1).astype(jnp.bfloat16), "fsdp", swaps(4, 1))
    cross = lax.ppermute(of_member(3).astype(jnp.bfloat16), "fsdp", swaps(4, 1))
    outward = (of_member(2) + cross.astype(jnp.float32)).astype(jnp.bfloat16)
    far = lax.ppermute(outward, "fsdp", swaps(4, 2))
    mine = (of_member(0) + near.astype(jnp.float32) + far.astype(jnp.float32)).astype(jnp.bfloat16)
    rows = block // c_count
    pieces = []
    for step in range(c_count):
        piece = lax.dynamic_slice_in_dim(mine, (c_place ^ step) * rows, rows, axis=0)
        pieces.append(lax.ppermute(piece, "context", swaps(4, step)) if step else piece)
    return jnp.concatenate(
        [pick(pieces, c_place ^ column).astype(jnp.float32) for column in range(c_count)], axis=1
    )


def gather_tokens(rows):
    return lax.all_gather(rows, ("context", "tensor"), axis=0, tiled=True)


def scatter_tokens(partial_sum):
    return lax.psum_scatter(
        partial_sum.astype(jnp.bfloat16), ("context", "tensor"), scatter_dimension=0, tiled=True
    ).astype(jnp.float32)


def pair_share(partial_sum):
    return lax.psum_scatter(
        partial_sum.astype(jnp.bfloat16), "tensor", scatter_dimension=0, tiled=True
    ).astype(jnp.float32)


def pair_join(share):
    return lax.all_gather(share.astype(jnp.bfloat16), "tensor", axis=0, tiled=True)


def times(left, right):
    return jnp.dot(left, right, preferred_element_type=jnp.float32)


def times_columns(left, right):
    return lax.dot_general(left, right, CONTRACT_COLS, preferred_element_type=jnp.float32)


def times_rows(left, right):
    return lax.dot_general(left, right, CONTRACT_ROWS, preferred_element_type=jnp.float32)


def shards(
    x_in,
    doc_lengths,
    w_query,
    key_weight,
    value_weight,
    output_weight,
    w_gate,
    w_up,
    w_down,
    norm_gains,
    grad_y,
):
    tok_rows, width = x_in.shape
    seq_len = tok_rows * lax.axis_size("context")
    heads_kv = key_weight.shape[1] // HEAD_SIZE
    query_groups = w_query.shape[1] // key_weight.shape[1]
    heads_q = heads_kv * query_groups
    kv_cols = heads_kv * HEAD_SIZE
    q_cols = heads_q * HEAD_SIZE
    key_block = 4 * tok_rows
    block_count = seq_len // key_block
    lengths = doc_lengths[0]
    query_tok = lax.axis_index("context") * tok_rows + jnp.arange(tok_rows, dtype=jnp.int32)
    key_tok = jnp.arange(seq_len, dtype=jnp.int32)
    query_seg, query_pos = segment_info(lengths, query_tok)
    key_seg, key_pos = segment_info(lengths, key_tok)
    cosine_table, sine_table = rope_tables(query_pos, HEAD_SIZE // 2)
    pair_rows = tok_rows // lax.axis_size("tensor")
    pair_start = lax.axis_index("tensor") * pair_rows
    normed1_rows, unused_inv = rms_unit(x_in.astype(jnp.float32))
    gate_weight, up_weight, down_weight = (
        fetch_hidden(w_gate),
        fetch_hidden(w_up),
        fetch_hidden(w_down),
    )
    gathered = lax.all_gather(
        jnp.concatenate(
            [w_query, key_weight, value_weight, jnp.pad(norm_gains, ((0, 0), (0, 124)))], axis=1
        ),
        ("fsdp", "context"),
        axis=0,
        tiled=True,
    )
    out_weight = lax.all_gather(output_weight, ("fsdp", "context"), axis=0, tiled=True)
    gain_full = gathered[:, q_cols + 2 * kv_cols : q_cols + 2 * kv_cols + 4]
    full_input = gathered[:, : q_cols + 2 * kv_cols]
    attention_input_rows = (
        normed1_rows * gain_full[:, 0].astype(jnp.float32)[None, :]
    ).astype(jnp.bfloat16)
    projected = times(attention_input_rows, full_input)
    projected_queries = projected[:, :q_cols]
    projected_keys = projected[:, q_cols : q_cols + kv_cols]
    proj_v = projected[:, q_cols + kv_cols :]
    gain_f = gain_full.astype(jnp.float32)
    query_rows_rotated = (
        apply_rotary(
            projected_queries.reshape(tok_rows, heads_q, HEAD_SIZE), cosine_table, sine_table
        )
        .astype(jnp.bfloat16)
        .reshape(tok_rows, heads_kv, query_groups, HEAD_SIZE)
    )
    keys_own = (
        apply_rotary(
            projected_keys.reshape(tok_rows, heads_kv, HEAD_SIZE), cosine_table, sine_table
        )
        .astype(jnp.bfloat16)
        .reshape(tok_rows, kv_cols)
    )
    values_own = proj_v.astype(jnp.bfloat16)
    kv_all = lax.all_gather(
        jnp.concatenate([keys_own, values_own], axis=1), "context", axis=0, tiled=True
    )
    key_all, value_all = kv_all[:, :kv_cols], kv_all[:, kv_cols:]
    key_view = key_all.reshape(block_count, key_block, heads_kv, HEAD_SIZE)
    value_view = value_all.reshape(block_count, key_block, heads_kv, HEAD_SIZE)
    seg_view = key_seg.reshape(block_count, key_block)
    tok_view = key_tok.reshape(block_count, key_block)

    def forward_step(running, block):
        key_rows, value_rows, key_seg_b, key_tok_b = block
        allowed = live_pairs(query_seg, query_tok, key_seg_b, key_tok_b)

        def compute(unused):
            capped = capped_scores(query_rows_rotated, key_rows)
            raw_weight = jnp.where(allowed[None, None], jnp.exp(capped - SOFT_CAP), 0.0)
            return (
                jnp.sum(raw_weight, axis=-1),
                jnp.einsum(
                    "hgqk,khd->qhgd",
                    raw_weight.astype(jnp.bfloat16),
                    value_rows,
                    preferred_element_type=jnp.float32,
                ),
            )

        added = compute(0)
        return ((running[0] + added[0], running[1] + added[1]), None)

    start_fwd = (
        jnp.zeros((heads_kv, query_groups, tok_rows), jnp.float32),
        jnp.zeros((tok_rows, heads_kv, query_groups, HEAD_SIZE), jnp.float32),
    )
    denom, accum = lax.scan(forward_step, start_fwd, (key_view, value_view, seg_view, tok_view))[0]
    attention_output_rows = (accum / jnp.transpose(denom, (2, 0, 1))[..., None]).astype(
        jnp.bfloat16
    )
    log_total = SOFT_CAP + jnp.log(denom)
    out_flat = attention_output_rows.reshape(tok_rows, q_cols)
    x_f32 = lax.dynamic_slice_in_dim(x_in, pair_start, pair_rows, axis=0).astype(jnp.float32)
    dy_f32 = lax.dynamic_slice_in_dim(grad_y, pair_start, pair_rows, axis=0).astype(jnp.float32)
    normed1, inv_rms1 = rms_unit(x_f32)
    branch = pair_share(times_columns(out_flat, out_weight))
    normed2, inv_rms2 = rms_unit(branch)
    resid = x_f32 + normed2 * gain_f[:, 1][None, :]
    normed3, inv_rms3 = rms_unit(resid)
    ffn_input = gather_tokens((normed3 * gain_f[:, 2][None, :]).astype(jnp.bfloat16))
    gate = times(ffn_input, gate_weight)
    upward = times(ffn_input, up_weight)
    gelu_value, gelu_slope = gelu_parts(gate)
    hidden = (gelu_value * upward).astype(jnp.bfloat16)
    mix = scatter_tokens(times_columns(hidden, down_weight))
    normed4, inv_rms4 = rms_unit(mix)
    y_out = pair_join(resid + normed4 * gain_f[:, 3][None, :])
    dgain4 = jnp.sum(dy_f32 * normed4, axis=0)
    dmix = gather_tokens(
        norm_back(dy_f32, normed4, inv_rms4, gain_f[:, 3]).astype(jnp.bfloat16)
    )
    dhidden = times(dmix, down_weight)
    dgate = (dhidden * upward * gelu_slope).astype(jnp.bfloat16)
    dupward = (dhidden * gelu_value).astype(jnp.bfloat16)
    dffn = scatter_tokens(times_columns(dgate, gate_weight) + times_columns(dupward, up_weight))
    grad_down = return_hidden(times_rows(dmix, hidden))
    grad_gate = return_hidden(times_rows(ffn_input, dgate))
    grad_up = return_hidden(times_rows(ffn_input, dupward))
    dgain3 = jnp.sum(dffn * normed3, axis=0)
    dresid = dy_f32 + norm_back(dffn, normed3, inv_rms3, gain_f[:, 2])
    dgain2 = jnp.sum(dresid * normed2, axis=0)
    branch_gradient = pair_join(norm_back(dresid, normed2, inv_rms2, gain_f[:, 1]))
    attention_output_gradient = times(branch_gradient, out_weight).reshape(
        tok_rows, heads_kv, query_groups, HEAD_SIZE
    )
    dattn_b = attention_output_gradient.astype(jnp.bfloat16)
    delta = jnp.transpose(
        jnp.sum(attention_output_gradient * attention_output_rows.astype(jnp.float32), axis=-1),
        (1, 2, 0),
    )

    def backward_step(running, block):
        key_rows, value_rows, key_seg_b, key_tok_b = block
        allowed = live_pairs(query_seg, query_tok, key_seg_b, key_tok_b)

        def compute(unused):
            capped = capped_scores(query_rows_rotated, key_rows)
            prob = jnp.where(allowed[None, None], jnp.exp(capped - log_total[..., None]), 0.0)
            dprob = jnp.einsum(
                "qhgd,khd->hgqk", dattn_b, value_rows, preferred_element_type=jnp.float32
            )
            dscore = prob * (dprob - delta[..., None])
            dscore_b = (dscore * (1.0 - (capped / SOFT_CAP) ** 2) * SCORE_SCALE).astype(
                jnp.bfloat16
            )
            prob_b = prob.astype(jnp.bfloat16)
            dquery = jnp.einsum(
                "hgqk,khd->qhgd", dscore_b, key_rows, preferred_element_type=jnp.float32
            )
            dkey = jnp.einsum(
                "hgqk,qhgd->khd", dscore_b, query_rows_rotated, preferred_element_type=jnp.float32
            )
            dvalue = jnp.einsum(
                "hgqk,qhgd->khd", prob_b, dattn_b, preferred_element_type=jnp.float32
            )
            return (
                dquery,
                jnp.concatenate(
                    [dkey.reshape(key_block, kv_cols), dvalue.reshape(key_block, kv_cols)], axis=1
                ),
            )

        dquery, kv_block = compute(0)
        return (running + dquery, kv_block)

    dqueries, kv_blocks = lax.scan(
        backward_step,
        jnp.zeros((tok_rows, heads_kv, query_groups, HEAD_SIZE), jnp.float32),
        (key_view, value_view, seg_view, tok_view),
    )
    kv_terms = kv_blocks.reshape(seq_len, 2 * kv_cols)
    kv_grads = lax.psum_scatter(
        kv_terms.astype(jnp.bfloat16), "context", scatter_dimension=0, tiled=True
    ).astype(jnp.float32)
    dq_in = (
        rotary_backward(dqueries.reshape(tok_rows, heads_q, HEAD_SIZE), cosine_table, sine_table)
        .astype(jnp.bfloat16)
        .reshape(tok_rows, q_cols)
    )
    key_input_gradient = (
        rotary_backward(
            kv_grads[:, :kv_cols].reshape(tok_rows, heads_kv, HEAD_SIZE), cosine_table, sine_table
        )
        .astype(jnp.bfloat16)
        .reshape(tok_rows, kv_cols)
    )
    value_input_gradient = kv_grads[:, kv_cols:].astype(jnp.bfloat16)
    input_gradients = jnp.concatenate(
        [dq_in, key_input_gradient, value_input_gradient], axis=1
    )
    dinput = pair_share(times_columns(input_gradients, full_input))
    dgain1 = jnp.sum(dinput * normed1, axis=0)
    grad_x = pair_join(dresid + norm_back(dinput, normed1, inv_rms1, gain_f[:, 0]))
    input_grads = lax.psum_scatter(
        times_rows(attention_input_rows, input_gradients).astype(jnp.bfloat16),
        ("fsdp", "context"),
        scatter_dimension=0,
        tiled=True,
    ).astype(jnp.float32)
    grad_query = input_grads[:, :q_cols]
    grad_key = input_grads[:, q_cols : q_cols + kv_cols]
    grad_value = input_grads[:, q_cols + kv_cols :]
    grad_out = lax.psum_scatter(
        times_rows(branch_gradient, out_flat).astype(jnp.bfloat16),
        ("fsdp", "context"),
        scatter_dimension=0,
        tiled=True,
    ).astype(jnp.float32)
    local_gains = jnp.stack([dgain1, dgain2, dgain3, dgain4], axis=1)
    grad_gains = lax.psum(
        lax.psum_scatter(local_gains, ("fsdp", "context"), scatter_dimension=0, tiled=True),
        "tensor",
    )
    return (
        y_out,
        grad_x,
        grad_query,
        grad_key,
        grad_value,
        grad_out,
        grad_gate,
        grad_up,
        grad_down,
        grad_gains,
    )


def solution(mesh):
    return jax.shard_map(
        shards,
        mesh=mesh,
        in_specs=(
            P(("fsdp", "context"), None),
            P("fsdp", None),
            P(("fsdp", "context"), "tensor"),
            P(("fsdp", "context"), "tensor"),
            P(("fsdp", "context"), "tensor"),
            P(("fsdp", "context"), "tensor"),
            P(("fsdp", "context"), "tensor"),
            P(("fsdp", "context"), "tensor"),
            P(("fsdp", "context"), "tensor"),
            P(("fsdp", "context"), None),
            P(("fsdp", "context"), None),
        ),
        out_specs=(
            P(("fsdp", "context"), None),
            P(("fsdp", "context"), None),
            P(("fsdp", "context"), "tensor"),
            P(("fsdp", "context"), "tensor"),
            P(("fsdp", "context"), "tensor"),
            P(("fsdp", "context"), "tensor"),
            P(("fsdp", "context"), "tensor"),
            P(("fsdp", "context"), "tensor"),
            P(("fsdp", "context"), "tensor"),
            P(("fsdp", "context"), None),
        ),
        check_vma=False,
    )
```
